256 devices in a mesh: tm: 8 (over z), row: 4 (over y), col: 8 (over x, core).
Axes of the slice: x: 4, y: 4, z: 8, core: 2. Of those that a mesh axis runs over, the one named last changes fastest.
Arguments:
- latent: bfloat16 [32, 64, 192, 256], P('tm', 'row', 'col'), may hold values from -43 to 43
- gain_first: float32 [256], replicated, may hold values from 0.5 to 1.5
- bias_first: float32 [256], replicated, may hold values from -3 to 3
- kernel_first: bfloat16 [3, 3, 3, 256, 256], replicated, may hold values from -0.078125 to 0.078125
- gain_second: float32 [256], replicated, may hold values from 0.5 to 1.5
- bias_second: float32 [256], replicated, may hold values from -3 to 3
- kernel_second: bfloat16 [3, 3, 3, 256, 256], replicated, may hold values from -0.078125 to 0.078125
- conv_bias: float32 [256], replicated, may hold values from -3 to 3
Outputs:
- upsampled: bfloat16 [32, 128, 384, 256], P('tm', 'row', 'col')
The draws below stay inside these ranges and needn't reach their ends.
All inputs are finite; a program needn't handle non-finite values.
Results may differ from the reference program's by a relative error of at most 0.006.
Values may be sent and summed in bfloat16 or wider, within the bound.
A program may use at most 64 MiB of HBM per device.

```python
import jax
import jax.numpy as jnp
from jax import lax

C = 256
GROUPS = 32
SPAN = 4
FRAMES = 32
HEIGHT = 64
WIDTH = 192
N_TM = 8


def draw_latent(key, part):
    keys = jax.random.split(key, 4)
    frame_pos = jnp.arange(FRAMES, dtype=jnp.float32) / float(max(FRAMES - 1, 1))
    frame_scale = 0.6 * jnp.exp(jnp.log(3.0) * frame_pos)
    channel_scale = jnp.exp(jax.random.uniform(keys[1], (C,), jnp.float32, jnp.log(0.3), jnp.log(3.0)))
    row_scale = jax.random.uniform(keys[2], (HEIGHT,), jnp.float32, 0.6, 1.4)
    col_scale = jax.random.uniform(keys[3], (WIDTH,), jnp.float32, 0.6, 1.4)
    base_values = jax.random.truncated_normal(keys[0], -4.0, 4.0, (FRAMES, HEIGHT, WIDTH, C), jnp.float32)
    values = base_values * frame_scale[:, None, None, None] * row_scale[:, None, None] * col_scale[:, None] * channel_scale
    return values.astype(jnp.bfloat16)


def normal_values(key, shape, deviation, reach, kind=jnp.bfloat16):
    return jnp.clip(deviation * jax.random.normal(key, shape, jnp.float32), -reach, reach).astype(kind)


def setup_inputs(seed: int = 0) -> dict:
    key_of = jax.random.split(jax.random.key(seed), 9)
    return {
        "latent": draw_latent(jax.random.fold_in(key_of[8], 71), 0),
        "gain_first": jnp.clip(jax.random.uniform(key_of[1], (C,), jnp.float32, 0.5, 1.5), 0.5, 1.5),
        "bias_first": normal_values(key_of[2], (C,), 0.5, 3.0, jnp.float32),
        "kernel_first": normal_values(key_of[3], (3, 3, 3, C, C), (27 * C) ** -0.5, 0.078125),
        "gain_second": jnp.clip(jax.random.uniform(key_of[4], (C,), jnp.float32, 0.5, 1.5), 0.5, 1.5),
        "bias_second": normal_values(key_of[5], (C,), 0.5, 3.0, jnp.float32),
        "kernel_second": normal_values(key_of[6], (3, 3, 3, C, C), (27 * C) ** -0.5, 0.078125),
        "conv_bias": normal_values(key_of[7], (C,), 0.5, 3.0, jnp.float32),
    }


EPSILON = 1e-06

def causal_norm(source, norm_gain, norm_bias):
    values = source.astype(jnp.float32)
    grouped = values.reshape(FRAMES, HEIGHT * WIDTH, GROUPS, C // GROUPS)
    frame_sum = lax.optimization_barrier(jnp.sum(grouped, axis=(1, 3)))
    frame_square = lax.optimization_barrier(jnp.sum(grouped * grouped, axis=(1, 3)))
    span_sum = jnp.cumsum(frame_sum.reshape(N_TM, SPAN, GROUPS).sum(1), 0)
    span_square = jnp.cumsum(frame_square.reshape(N_TM, SPAN, GROUPS).sum(1), 0)
    cell_count = (jnp.arange(N_TM, dtype=jnp.float32) + 1.0) * float(SPAN * HEIGHT * WIDTH * (C // GROUPS))
    group_mean = span_sum / cell_count[:, None]
    group_var = span_square / cell_count[:, None] - group_mean * group_mean
    norm_scale = lax.rsqrt(group_var + EPSILON)
    channel_mean = jnp.repeat(jnp.repeat(group_mean, SPAN, axis=0), C // GROUPS, axis=1)
    channel_scale = jnp.repeat(jnp.repeat(norm_scale, SPAN, axis=0), C // GROUPS, axis=1)
    normed = (values - channel_mean[:, None, None, :]) * (channel_scale * norm_gain)[:, None, None, :] + norm_bias
    return jax.nn.silu(normed).astype(jnp.bfloat16)

def causal_conv(activated, kernel):
    padded = jnp.pad(activated, ((2, 0), (1, 1), (1, 1), (0, 0)))

    def one_frame(frame_pos):
        frame_slab = lax.dynamic_slice_in_dim(padded, frame_pos, 3, 0)
        running = jnp.zeros((HEIGHT * WIDTH, C), jnp.float32)
        for tap_row in range(3):
            for tap_col in range(3):
                window = frame_slab[:, tap_row:tap_row + HEIGHT, tap_col:tap_col + WIDTH, :]
                stacked = jnp.transpose(window, (1, 2, 0, 3)).reshape(HEIGHT * WIDTH, 3 * C)
                running = running + jnp.dot(stacked, kernel[:, tap_row, tap_col].reshape(3 * C, C), preferred_element_type=jnp.float32)
        return running.reshape(HEIGHT, WIDTH, C)
    return lax.map(one_frame, jnp.arange(FRAMES, dtype=jnp.int32))

def reference(latent, gain_first, bias_first, kernel_first, gain_second, bias_second, kernel_second, conv_bias):
    act_first = causal_norm(latent, gain_first, bias_first)
    hidden = causal_conv(act_first, kernel_first).astype(jnp.bfloat16)
    act_second = causal_norm(hidden, gain_second, bias_second)
    branch = causal_conv(act_second, kernel_second)
    summed = (latent.astype(jnp.float32) + branch + conv_bias).astype(jnp.bfloat16)
    return jnp.repeat(jnp.repeat(summed, 2, axis=1), 2, axis=2)
```

```python
import functools

import jax
import jax.numpy as jnp
from jax import lax
from jax.experimental import pallas as pl
from jax.experimental.pallas import tpu as pltpu
from jax.sharding import PartitionSpec as P

GROUPS = 32
EPSILON = 1e-06
MESH = pl.DeviceIdType.MESH
F32 = jnp.float32
BF16 = jnp.bfloat16


def lane_of(shape):
    return lax.broadcasted_iota(jnp.int32, shape, 1) % 8


def group_total(x):
    lane = lane_of(x.shape)
    lanes = x.shape[1]
    for step in (1, 2, 4):
        above = pltpu.roll(x, lanes - step, 1)
        below = pltpu.roll(x, step, 1)
        x = x + jnp.where((lane // step) % 2 == 0, above, below)
    return x


def pack_moments(total, square):
    rows = jnp.concatenate([total[:, :128], total[:, 128:], square[:, :128], square[:, 128:]], axis=0)
    rows = group_total(rows)
    lane = lane_of((1, 128))
    row = jnp.zeros((1, 128), F32)
    for k in range(4):
        row = jnp.where(lane == k, rows[k : k + 1], row)
    return row


def unpack_moments(row):
    lane = lane_of((1, 128))
    rows = jnp.concatenate([jnp.where(lane == k, row, 0.0) for k in range(4)], axis=0)
    rows = group_total(rows)
    total = jnp.concatenate([rows[0:1], rows[1:2]], axis=1)
    square = jnp.concatenate([rows[2:3], rows[3:4]], axis=1)
    return total, square


def half_terms(row, count, gain, bias):
    total, square = unpack_moments(row)
    mean = total / count
    scale = lax.rsqrt(square / count - mean * mean + EPSILON) * gain
    return 0.5 * scale, 0.5 * (bias - mean * scale)


def silu_of(x, scale, offset):
    u = x * scale + offset
    return u + u * jnp.tanh(u)


def build(x_ref, col_ref, act_ref, edge_ref, terms_ref, first, last, before, marks):
    north, south, west, east = marks
    rows = x_ref.shape[1]
    cols = x_ref.shape[2]
    scale = terms_ref[2 * before : 2 * before + 1, :]
    offset = terms_ref[2 * before + 1 : 2 * before + 2, :]
    at = lax.broadcasted_iota(jnp.int32, (col_ref.shape[2], 1), 0)
    inside = jnp.where(at == 0, north, jnp.where(at == rows - 1, south, 1.0))
    place = lax.broadcasted_iota(jnp.int32, (cols, 1), 0)

    @pl.loop(first, last)
    def _(t):
        for side, mark in ((0, west), (1, east)):
            keep = inside * mark
            edge_ref[side] = silu_of(col_ref[side, t].astype(F32), scale * keep, offset * keep)
        for h in range(rows):
            keep = north if h == 0 else south if h == rows - 1 else None
            s, o = (scale, offset) if keep is None else (scale * keep, offset * keep)
            z = silu_of(x_ref[t, h].astype(F32), s, o)
            act_ref[1, t, h] = z.astype(BF16)
            left = jnp.where(place == 0, edge_ref[0, h : h + 1, :], pltpu.roll(z, 1, 0))
            act_ref[0, t, h] = left.astype(BF16)
            right = jnp.where(place == cols - 1, edge_ref[1, h : h + 1, :], pltpu.roll(z, cols - 1, 0))
            act_ref[2, t, h] = right.astype(BF16)


def conv_frame(act_ref, w_ref, t):
    _, _, rows, cols, channels = act_ref.shape
    rows = rows - 2
    out = jnp.zeros((rows * cols, w_ref.shape[-1]), F32)
    for a in range(3):
        for b in range(3):
            for e in range(3):
                x = act_ref[e, t + a, b : b + rows].reshape(rows * cols, channels)
                out = out + jnp.dot(x, w_ref[(a * 3 + b) * 3 + e], preferred_element_type=F32)
    return out


def sums_of(x):
    parts = x.reshape(-1, 8, x.shape[-1])
    return jnp.sum(parts, axis=0), jnp.sum(parts * parts, axis=0)


def marks_of(n_row, n_col):
    row, col = lax.axis_index("row"), lax.axis_index("col")
    one, zero = jnp.float32(1.0), jnp.float32(0.0)
    return (
        jnp.where(row == 0, zero, one),
        jnp.where(row == n_row - 1, zero, one),
        jnp.where(col == 0, zero, one),
        jnp.where(col == n_col - 1, zero, one),
    )


def first_kernel(
    sizes, count,
    lat_hbm, w1_hbm, w2_hbm, gain1_hbm, bias1_hbm, gain2_hbm, bias2_hbm,
    xl, xh, colh, w2, terms2,
    act, w1, coll, send_l, send_h, edge, pick, affine, terms1,
    sum_send, plane_in, tm_send, tm_in,
    load_sem, send_sem, recv_sem, sum_send_sem, sum_recv_sem,
):
    n_tm, n_row, n_col = sizes
    tm, row, col = lax.axis_index("tm"), lax.axis_index("row"), lax.axis_index("col")
    frames, rows, cols = xl.shape[0] - 2, xl.shape[1] - 2, xl.shape[2]
    plane = n_row * n_col
    mine = row * n_col + col
    marks = marks_of(n_row, n_col)

    loads = [
        pltpu.make_async_copy(lat_hbm, xl.at[2:, 1 : rows + 1], load_sem.at[0]),
        pltpu.make_async_copy(gain1_hbm, affine.at[0], load_sem.at[1]),
        pltpu.make_async_copy(bias1_hbm, affine.at[1], load_sem.at[2]),
        pltpu.make_async_copy(gain2_hbm, affine.at[2], load_sem.at[3]),
        pltpu.make_async_copy(bias2_hbm, affine.at[3], load_sem.at[4]),
        pltpu.make_async_copy(w1_hbm, w1, load_sem.at[5]),
        pltpu.make_async_copy(w2_hbm, w2, load_sem.at[6]),
    ]
    for load in loads:
        load.start()

    def plane_peer(d):
        at = lax.rem(mine + d, plane)
        return (tm, at // n_col, lax.rem(at, n_col))

    def tm_peer(d):
        return (lax.rem(tm + d, n_tm), row, col)

    barrier = pltpu.get_barrier_semaphore()

    @pl.loop(1, plane)
    def _(d):
        pl.semaphore_signal(barrier, inc=1, device_id=plane_peer(d), device_id_type=MESH)

    @pl.loop(1, n_tm)
    def _(d):
        pl.semaphore_signal(barrier, inc=1, device_id=tm_peer(d), device_id_type=MESH)

    pick[...] = jnp.zeros_like(pick)
    north = (tm, lax.rem(row + n_row - 1, n_row), col)
    south = (tm, lax.rem(row + 1, n_row), col)
    west = (tm, row, lax.rem(col + n_col - 1, n_col))
    east = (tm, row, lax.rem(col + 1, n_col))
    later = tm_peer(1)

    def remote(src, dst, which, device):
        copy = pltpu.make_async_remote_copy(
            src_ref=src, dst_ref=dst, send_sem=send_sem.at[which], recv_sem=recv_sem.at[which],
            device_id=device, device_id_type=MESH,
        )
        copy.start()
        return copy

    def send_plane(which, moments):
        sum_send[which] = moments

        @pl.loop(1, plane)
        def _(d):
            pltpu.make_async_remote_copy(
                src_ref=sum_send.at[which], dst_ref=plane_in.at[which, d - 1],
                send_sem=sum_send_sem.at[which], recv_sem=sum_recv_sem.at[which],
                device_id=plane_peer(d), device_id_type=MESH,
            ).start()

    def all_plane(which):
        pltpu.make_async_copy(plane_in.at[which], plane_in.at[which], sum_recv_sem.at[which]).wait()
        return sum_send[which] + jnp.sum(plane_in[which], axis=0)

    def send_tm(which, moments):
        tm_send[which] = moments

        @pl.loop(1, n_tm)
        def _(d):
            pltpu.make_async_remote_copy(
                src_ref=tm_send.at[which], dst_ref=tm_in.at[which, d - 1],
                send_sem=sum_send_sem.at[2 + which], recv_sem=sum_recv_sem.at[2 + which],
                device_id=tm_peer(d), device_id_type=MESH,
            ).start()

    def all_tm(which, terms):
        pltpu.make_async_copy(tm_in.at[which], tm_in.at[which], sum_recv_sem.at[2 + which]).wait()
        prior = jnp.zeros((1, 128), F32)
        for d in range(1, n_tm):
            prior = prior + jnp.where(tm >= d, tm_in[which, d - 1], 0.0)
        upto = prior + tm_send[which]
        done = tm.astype(F32)
        gain, bias = affine[2 * which], affine[2 * which + 1]
        scale, offset = half_terms(upto, (done + 1.0) * count, gain, bias)
        terms[0:1, :] = scale
        terms[1:2, :] = offset
        scale, offset = half_terms(prior, jnp.maximum(done, 1.0) * count, gain, bias)
        keep = jnp.where(tm == 0, jnp.float32(0.0), jnp.float32(1.0))
        terms[2:3, :] = scale * keep
        terms[3:4, :] = offset * keep

    def sums_sent(which):
        pltpu.make_async_copy(plane_in.at[which], plane_in.at[which], sum_send_sem.at[which]).wait()
        pltpu.make_async_copy(tm_in.at[which], tm_in.at[which], sum_send_sem.at[2 + which]).wait()

    def columns(x, out):
        for side, lo, at in ((0, cols - 8, 7), (1, 0, 0)):
            @pl.loop(2, frames + 2)
            def _(t):
                for h in range(rows + 2):
                    tile = x[t, h, lo : lo + 8, :].astype(F32)
                    pick[h : h + 1, :] = tile[at : at + 1, :]
                out[side, t - 2] = pick[...].astype(BF16)

    def halo_rows(x, base, lo, hi):
        return [
            remote(x.at[lo:hi, 1], x.at[lo:hi, rows + 1], base, north),
            remote(x.at[lo:hi, rows], x.at[lo:hi, 0], base + 1, south),
        ]

    def halo_columns(out, cells, base):
        return [
            remote(out.at[0], cells.at[0, 2:], base, east),
            remote(out.at[1], cells.at[1, 2:], base + 1, west),
        ]

    def onward_rows(x, base):
        return [
            remote(x.at[frames : frames + 2, 0], x.at[0:2, 0], base, later),
            remote(x.at[frames : frames + 2, rows + 1], x.at[0:2, rows + 1], base + 1, later),
        ]

    def onward_columns(cells, base):
        return [
            remote(cells.at[0, frames : frames + 2], cells.at[0, 0:2], base, later),
            remote(cells.at[1, frames : frames + 2], cells.at[1, 0:2], base + 1, later),
        ]

    def onward_frames(x, which):
        return [remote(x.at[frames : frames + 2, 1 : rows + 1], x.at[0:2, 1 : rows + 1], which, later)]

    loads[0].wait()

    def add_frame(t, so_far):
        s, q = sums_of(xl[t, 1 : rows + 1].reshape(rows * cols, -1).astype(F32))
        return so_far[0] + s, so_far[1] + q

    none = jnp.zeros((8, xl.shape[-1]), F32)
    s, q = lax.fori_loop(2, frames + 2, add_frame, (none, none))
    moments = pack_moments(jnp.sum(s, axis=0, keepdims=True), jnp.sum(q, axis=0, keepdims=True))
    pl.semaphore_wait(barrier, plane - 1 + n_tm - 1)

    send_plane(0, moments)
    by_row = halo_rows(xl, 0, 2, frames + 2)
    onward = onward_frames(xl, 2)
    for copy in by_row:
        copy.wait_recv()
    columns(xl, send_l)
    by_col = halo_columns(send_l, coll, 3)
    onward += onward_rows(xl, 5)
    moments = all_plane(0)
    send_tm(0, moments)
    for copy in by_col:
        copy.wait_recv()
    onward += onward_columns(coll, 7)
    for load in loads[1:5]:
        load.wait()
    all_tm(0, terms1)

    build(xl, coll, act, edge, terms1, 2, frames + 2, 0, marks)
    loads[5].wait()

    def hidden_frame(t, so_far):
        h = conv_frame(act, w1, t).astype(BF16)
        xh[t + 2, 1 : rows + 1] = h.reshape(rows, cols, -1)
        s, q = sums_of(h.astype(F32))
        return so_far[0] + s, so_far[1] + q

    sums = lax.fori_loop(frames - 2, frames, hidden_frame, (none, none))
    onward2 = onward_frames(xh, 9)
    by_row2 = halo_rows(xh, 10, frames, frames + 2)
    for copy in onward:
        copy.wait_recv()
    build(xl, coll, act, edge, terms1, 0, 2, 1, marks)
    s, q = lax.fori_loop(0, frames - 2, hidden_frame, sums)
    moments = pack_moments(jnp.sum(s, axis=0, keepdims=True), jnp.sum(q, axis=0, keepdims=True))
    send_plane(1, moments)
    by_row2 += halo_rows(xh, 12, 2, frames)
    for copy in by_row2:
        copy.wait_recv()
    columns(xh, send_h)
    by_col2 = halo_columns(send_h, colh, 14)
    onward2 += onward_rows(xh, 16)
    moments = all_plane(1)
    send_tm(1, moments)
    for copy in by_col2:
        copy.wait_recv()
    onward2 += onward_columns(colh, 18)
    all_tm(1, terms2)
    loads[6].wait()
    for copy in onward2:
        copy.wait_recv()
    for copy in by_row + by_col + onward + by_row2 + by_col2 + onward2:
        copy.wait_send()
    sums_sent(0)
    sums_sent(1)


N_COPIES = 20


def second_kernel(
    sizes, xl, xh, colh, w2, terms2, bias_ref, out_hbm, act, edge, wide, stage, out_sem
):
    n_tm, n_row, n_col = sizes
    marks = marks_of(n_row, n_col)
    frames, rows, cols = xl.shape[0] - 2, xl.shape[1] - 2, xl.shape[2]
    build(xh, colh, act, edge, terms2, 2, frames + 2, 0, marks)
    build(xh, colh, act, edge, terms2, 0, 2, 1, marks)

    def stores(t):
        return [
            pltpu.make_async_copy(stage.at[t], out_hbm.at[t, :, k], out_sem.at[t, k]) for k in range(2)
        ]

    for t in range(frames):
        y = conv_frame(act, w2, t) + bias_ref[...]
        y = y + xl[t + 2, 1 : rows + 1].reshape(rows * cols, -1).astype(F32)
        for half in range(2):
            part = y[:, 128 * half : 128 * half + 128]
            wide[t % 2, half, pl.ds(0, rows * cols, stride=2), :] = part
            wide[t % 2, half, pl.ds(1, rows * cols, stride=2), :] = part
        for half in range(2):
            stage[t, :, :, 128 * half : 128 * half + 128] = (
                wide[t % 2, half].astype(BF16).reshape(rows, 2 * cols, 128)
            )
        for copy in stores(t):
            copy.start()
    for t in range(frames):
        for copy in stores(t):
            copy.wait()


def on_device(sizes, latent, gain_first, bias_first, kernel_first, gain_second, bias_second, kernel_second, conv_bias):
    n_tm, n_row, n_col = sizes
    frames, rows, cols, channels = latent.shape
    plane = n_row * n_col
    per_span = float(frames * rows * n_row * cols * n_col * (channels // GROUPS))
    tile = (frames + 2, rows + 2, cols, channels)
    tall = -(-(rows + 2) // 8) * 8
    cells = (2, frames + 2, tall, channels)
    send = (2, frames, tall, channels)
    taps = (27, channels, channels)
    anywhere = pl.BlockSpec(memory_space=pl.ANY)
    inside = pl.BlockSpec(memory_space=pltpu.VMEM)
    kept = [
        pltpu.VMEM(tile, BF16),
        pltpu.VMEM(tile, BF16),
        pltpu.VMEM(cells, BF16),
        pltpu.VMEM(taps, BF16),
        pltpu.VMEM((8, channels), F32),
    ]
    held = pl.pallas_call(
        functools.partial(first_kernel, sizes, per_span),
        out_shape=kept,
        in_specs=[anywhere] * 7,
        out_specs=[inside] * 5,
        scratch_shapes=[
            pltpu.VMEM((3, *tile), BF16),
            pltpu.VMEM(taps, BF16),
            pltpu.VMEM(cells, BF16),
            pltpu.VMEM(send, BF16),
            pltpu.VMEM(send, BF16),
            pltpu.VMEM((2, tall, channels), F32),
            pltpu.VMEM((tall, channels), F32),
            pltpu.VMEM((4, 1, channels), F32),
            pltpu.VMEM((8, channels), F32),
            pltpu.VMEM((2, 1, 128), F32),
            pltpu.VMEM((2, plane - 1, 1, 128), F32),
            pltpu.VMEM((2, 1, 128), F32),
            pltpu.VMEM((2, n_tm - 1, 1, 128), F32),
            pltpu.SemaphoreType.DMA((7,)),
            pltpu.SemaphoreType.DMA((N_COPIES,)),
            pltpu.SemaphoreType.DMA((N_COPIES,)),
            pltpu.SemaphoreType.DMA((4,)),
            pltpu.SemaphoreType.DMA((4,)),
        ],
        compiler_params=pltpu.CompilerParams(
            collective_id=0, has_side_effects=True, vmem_limit_bytes=24 * 2**20
        ),
        name="first_conv",
    )(
        latent,
        kernel_first.reshape(taps),
        kernel_second.reshape(taps),
        gain_first.reshape(1, channels),
        bias_first.reshape(1, channels),
        gain_second.reshape(1, channels),
        bias_second.reshape(1, channels),
    )
    out = pl.pallas_call(
        functools.partial(second_kernel, sizes),
        out_shape=jax.ShapeDtypeStruct((frames, rows, 2, 2 * cols, channels), BF16),
        in_specs=[inside] * 6,
        out_specs=anywhere,
        scratch_shapes=[
            pltpu.VMEM((3, *tile), BF16),
            pltpu.VMEM((2, tall, channels), F32),
            pltpu.VMEM((2, 2, 2 * rows * cols, 128), F32),
            pltpu.VMEM((frames, rows, 2 * cols, channels), BF16),
            pltpu.SemaphoreType.DMA((frames, 2)),
        ],
        compiler_params=pltpu.CompilerParams(vmem_limit_bytes=24 * 2**20),
        name="second_conv",
    )(*held, conv_bias.reshape(1, channels))
    return out.reshape(frames, 2 * rows, 2 * cols, channels)


def solution(mesh):
    sizes = (mesh.shape["tm"], mesh.shape["row"], mesh.shape["col"])
    return jax.shard_map(
        functools.partial(on_device, sizes),
        mesh=mesh,
        in_specs=(P("tm", "row", "col", None), P(), P(), P(), P(), P(), P(), P()),
        out_specs=P("tm", "row", "col", None),
        check_vma=False,
    )
```

```python
import functools

import jax
import jax.numpy as jnp
from jax import lax
from jax.experimental import pallas as pl
from jax.experimental.pallas import tpu as pltpu
from jax.sharding import PartitionSpec as P

GROUPS = 32
EPSILON = 1e-06
MESH = pl.DeviceIdType.MESH
F32 = jnp.float32
BF16 = jnp.bfloat16


def lane_of(shape):
    return lax.broadcasted_iota(jnp.int32, shape, 1) % 8


def group_total(x):
    lane = lane_of(x.shape)
    lanes = x.shape[1]
    for step in (1, 2, 4):
        above = pltpu.roll(x, lanes - step, 1)
        below = pltpu.roll(x, step, 1)
        x = x + jnp.where((lane // step) % 2 == 0, above, below)
    return x


def pack_moments(total, square):
    rows = jnp.concatenate([total[:, :128], total[:, 128:], square[:, :128], square[:, 128:]], axis=0)
    rows = group_total(rows)
    lane = lane_of((1, 128))
    row = jnp.zeros((1, 128), F32)
    for k in range(4):
        row = jnp.where(lane == k, rows[k : k + 1], row)
    return row


def unpack_moments(row):
    lane = lane_of((1, 128))
    rows = jnp.concatenate([jnp.where(lane == k, row, 0.0) for k in range(4)], axis=0)
    rows = group_total(rows)
    total = jnp.concatenate([rows[0:1], rows[1:2]], axis=1)
    square = jnp.concatenate([rows[2:3], rows[3:4]], axis=1)
    return total, square


def half_terms(row, count, gain, bias):
    total, square = unpack_moments(row)
    mean = total / count
    scale = lax.rsqrt(square / count - mean * mean + EPSILON) * gain
    return 0.5 * scale, 0.5 * (bias - mean * scale)


def silu_of(x, scale, offset):
    u = x * scale + offset
    return u + u * jnp.tanh(u)


def build(x_ref, col_ref, act_ref, edge_ref, terms_ref, first, last, before, marks):
    north, south, west, east = marks
    rows = x_ref.shape[1]
    cols = x_ref.shape[2]
    scale = terms_ref[2 * before : 2 * before + 1, :]
    offset = terms_ref[2 * before + 1 : 2 * before + 2, :]
    at = lax.broadcasted_iota(jnp.int32, (col_ref.shape[2], 1), 0)
    inside = jnp.where(at == 0, north, jnp.where(at == rows - 1, south, 1.0))
    place = lax.broadcasted_iota(jnp.int32, (cols, 1), 0)

    @pl.loop(first, last)
    def _(t):
        for side, mark in ((0, west), (1, east)):
            keep = inside * mark
            edge_ref[side] = silu_of(col_ref[side, t].astype(F32), scale * keep, offset * keep)
        for h in range(rows):
            keep = north if h == 0 else south if h == rows - 1 else None
            s, o = (scale, offset) if keep is None else (scale * keep, offset * keep)
            z = silu_of(x_ref[t, h].astype(F32), s, o)
            act_ref[1, t, h] = z.astype(BF16)
            left = jnp.where(place == 0, edge_ref[0, h : h + 1, :], pltpu.roll(z, 1, 0))
            act_ref[0, t, h] = left.astype(BF16)
            right = jnp.where(place == cols - 1, edge_ref[1, h : h + 1, :], pltpu.roll(z, cols - 1, 0))
            act_ref[2, t, h] = right.astype(BF16)


def conv_frame(act_ref, w_ref, t):
    _, _, rows, cols, channels = act_ref.shape
    rows = rows - 2
    out = jnp.zeros((rows * cols, w_ref.shape[-1]), F32)
    for a in range(3):
        for b in range(3):
            for e in range(3):
                x = act_ref[e, t + a, b : b + rows].reshape(rows * cols, channels)
                out = out + jnp.dot(x, w_ref[(a * 3 + b) * 3 + e], preferred_element_type=F32)
    return out


def sums_of(x):
    parts = x.reshape(-1, 8, x.shape[-1])
    return jnp.sum(parts, axis=0), jnp.sum(parts * parts, axis=0)


def marks_of(n_row, n_col):
    row, col = lax.axis_index("row"), lax.axis_index("col")
    one, zero = jnp.float32(1.0), jnp.float32(0.0)
    return (
        jnp.where(row == 0, zero, one),
        jnp.where(row == n_row - 1, zero, one),
        jnp.where(col == 0, zero, one),
        jnp.where(col == n_col - 1, zero, one),
    )


def first_kernel(
    sizes, count,
    lat_hbm, w1_hbm, w2_hbm, gain1_hbm, bias1_hbm, gain2_hbm, bias2_hbm,
    xl, xh, colh, w2, terms2,
    act, w1, coll, send_l, send_h, edge, pick, affine, terms1,
    sum_send, plane_in, tm_send, tm_in,
    load_sem, send_sem, recv_sem, sum_send_sem, sum_recv_sem,
):
    n_tm, n_row, n_col = sizes
    tm, row, col = lax.axis_index("tm"), lax.axis_index("row"), lax.axis_index("col")
    frames, rows, cols = xl.shape[0] - 2, xl.shape[1] - 2, xl.shape[2]
    plane = n_row * n_col
    mine = row * n_col + col
    marks = marks_of(n_row, n_col)

    loads = [
        pltpu.make_async_copy(lat_hbm, xl.at[2:, 1 : rows + 1], load_sem.at[0]),
        pltpu.make_async_copy(gain1_hbm, affine.at[0], load_sem.at[1]),
        pltpu.make_async_copy(bias1_hbm, affine.at[1], load_sem.at[2]),
        pltpu.make_async_copy(gain2_hbm, affine.at[2], load_sem.at[3]),
        pltpu.make_async_copy(bias2_hbm, affine.at[3], load_sem.at[4]),
        pltpu.make_async_copy(w1_hbm, w1, load_sem.at[5]),
        pltpu.make_async_copy(w2_hbm, w2, load_sem.at[6]),
    ]
    for load in loads:
        load.start()

    def plane_peer(d):
        at = lax.rem(mine + d, plane)
        return (tm, at // n_col, lax.rem(at, n_col))

    def tm_peer(d):
        return (lax.rem(tm + d, n_tm), row, col)

    barrier = pltpu.get_barrier_semaphore()

    @pl.loop(1, plane)
    def _(d):
        pl.semaphore_signal(barrier, inc=1, device_id=plane_peer(d), device_id_type=MESH)

    @pl.loop(1, n_tm)
    def _(d):
        pl.semaphore_signal(barrier, inc=1, device_id=tm_peer(d), device_id_type=MESH)

    pick[...] = jnp.zeros_like(pick)
    north = (tm, lax.rem(row + n_row - 1, n_row), col)
    south = (tm, lax.rem(row + 1, n_row), col)
    west = (tm, row, lax.rem(col + n_col - 1, n_col))
    east = (tm, row, lax.rem(col + 1, n_col))
    later = tm_peer(1)

    def remote(src, dst, which, device):
        copy = pltpu.make_async_remote_copy(
            src_ref=src, dst_ref=dst, send_sem=send_sem.at[which], recv_sem=recv_sem.at[which],
            device_id=device, device_id_type=MESH,
        )
        copy.start()
        return copy

    def send_plane(which, moments):
        sum_send[which] = moments

        @pl.loop(1, plane)
        def _(d):
            pltpu.make_async_remote_copy(
                src_ref=sum_send.at[which], dst_ref=plane_in.at[which, d - 1],
                send_sem=sum_send_sem.at[which], recv_sem=sum_recv_sem.at[which],
                device_id=plane_peer(d), device_id_type=MESH,
            ).start()

    def all_plane(which):
        pltpu.make_async_copy(plane_in.at[which], plane_in.at[which], sum_recv_sem.at[which]).wait()
        return sum_send[which] + jnp.sum(plane_in[which], axis=0)

    def send_tm(which, moments):
        tm_send[which] = moments

        @pl.loop(1, n_tm)
        def _(d):
            pltpu.make_async_remote_copy(
                src_ref=tm_send.at[which], dst_ref=tm_in.at[which, d - 1],
                send_sem=sum_send_sem.at[2 + which], recv_sem=sum_recv_sem.at[2 + which],
                device_id=tm_peer(d), device_id_type=MESH,
            ).start()

    def all_tm(which, terms):
        pltpu.make_async_copy(tm_in.at[which], tm_in.at[which], sum_recv_sem.at[2 + which]).wait()
        prior = jnp.zeros((1, 128), F32)
        for d in range(1, n_tm):
            prior = prior + jnp.where(tm >= d, tm_in[which, d - 1], 0.0)
        upto = prior + tm_send[which]
        done = tm.astype(F32)
        gain, bias = affine[2 * which], affine[2 * which + 1]
        scale, offset = half_terms(upto, (done + 1.0) * count, gain, bias)
        terms[0:1, :] = scale
        terms[1:2, :] = offset
        scale, offset = half_terms(prior, jnp.maximum(done, 1.0) * count, gain, bias)
        keep = jnp.where(tm == 0, jnp.float32(0.0), jnp.float32(1.0))
        terms[2:3, :] = scale * keep
        terms[3:4, :] = offset * keep

    def sums_sent(which):
        pltpu.make_async_copy(plane_in.at[which], plane_in.at[which], sum_send_sem.at[which]).wait()
        pltpu.make_async_copy(tm_in.at[which], tm_in.at[which], sum_send_sem.at[2 + which]).wait()

    def columns(x, out):
        for side, lo, at in ((0, cols - 8, 7), (1, 0, 0)):
            @pl.loop(2, frames + 2)
            def _(t):
                for h in range(rows + 2):
                    tile = x[t, h, lo : lo + 8, :].astype(F32)
                    pick[h : h + 1, :] = tile[at : at + 1, :]
                out[side, t - 2] = pick[...].astype(BF16)

    def halo_rows(x, base, lo, hi):
        return [
            remote(x.at[lo:hi, 1], x.at[lo:hi, rows + 1], base, north),
            remote(x.at[lo:hi, rows], x.at[lo:hi, 0], base + 1, south),
        ]

    def halo_columns(out, cells, base):
        return [
            remote(out.at[0], cells.at[0, 2:], base, east),
            remote(out.at[1], cells.at[1, 2:], base + 1, west),
        ]

    def onward_rows(x, base):
        return [
            remote(x.at[frames : frames + 2, 0], x.at[0:2, 0], base, later),
            remote(x.at[frames : frames + 2, rows + 1], x.at[0:2, rows + 1], base + 1, later),
        ]

    def onward_columns(cells, base):
        return [
            remote(cells.at[0, frames : frames + 2], cells.at[0, 0:2], base, later),
            remote(cells.at[1, frames : frames + 2], cells.at[1, 0:2], base + 1, later),
        ]

    def onward_frames(x, which):
        return [remote(x.at[frames : frames + 2, 1 : rows + 1], x.at[0:2, 1 : rows + 1], which, later)]

    loads[0].wait()

    def add_frame(t, so_far):
        s, q = sums_of(xl[t, 1 : rows + 1].reshape(rows * cols, -1).astype(F32))
        return so_far[0] + s, so_far[1] + q

    none = jnp.zeros((8, xl.shape[-1]), F32)
    s, q = lax.fori_loop(2, frames + 2, add_frame, (none, none))
    moments = pack_moments(jnp.sum(s, axis=0, keepdims=True), jnp.sum(q, axis=0, keepdims=True))
    pl.semaphore_wait(barrier, plane - 1 + n_tm - 1)

    send_plane(0, moments)
    by_row = halo_rows(xl, 0, 2, frames + 2)
    onward = onward_frames(xl, 2)
    for copy in by_row:
        copy.wait_recv()
    columns(xl, send_l)
    by_col = halo_columns(send_l, coll, 3)
    onward += onward_rows(xl, 5)
    moments = all_plane(0)
    send_tm(0, moments)
    for copy in by_col:
        copy.wait_recv()
    onward += onward_columns(coll, 7)
    for load in loads[1:5]:
        load.wait()
    all_tm(0, terms1)

    build(xl, coll, act, edge, terms1, 2, frames + 2, 0, marks)
    loads[5].wait()

    def hidden_frame(t, so_far):
        h = conv_frame(act, w1, t).astype(BF16)
        xh[t + 2, 1 : rows + 1] = h.reshape(rows, cols, -1)
        s, q = sums_of(h.astype(F32))
        return so_far[0] + s, so_far[1] + q

    sums = lax.fori_loop(frames - 2, frames, hidden_frame, (none, none))
    onward2 = onward_frames(xh, 9)
    by_row2 = halo_rows(xh, 10, frames, frames + 2)
    for copy in onward:
        copy.wait_recv()
    build(xl, coll, act, edge, terms1, 0, 2, 1, marks)
    s, q = lax.fori_loop(0, frames - 2, hidden_frame, sums)
    moments = pack_moments(jnp.sum(s, axis=0, keepdims=True), jnp.sum(q, axis=0, keepdims=True))
    send_plane(1, moments)
    by_row2 += halo_rows(xh, 12, 2, frames)
    for copy in by_row2:
        copy.wait_recv()
    columns(xh, send_h)
    by_col2 = halo_columns(send_h, colh, 14)
    onward2 += onward_rows(xh, 16)
    moments = all_plane(1)
    send_tm(1, moments)
    for copy in by_col2:
        copy.wait_recv()
    onward2 += onward_columns(colh, 18)
    all_tm(1, terms2)
    loads[6].wait()
    for copy in onward2:
        copy.wait_recv()
    for copy in by_row + by_col + onward + by_row2 + by_col2 + onward2:
        copy.wait_send()
    sums_sent(0)
    sums_sent(1)


N_COPIES = 20


def second_kernel(
    sizes, xl, xh, colh, w2, terms2, bias_ref, out_hbm, act, edge, wide, stage, out_sem
):
    n_tm, n_row, n_col = sizes
    marks = marks_of(n_row, n_col)
    frames, rows, cols = xl.shape[0] - 2, xl.shape[1] - 2, xl.shape[2]
    build(xh, colh, act, edge, terms2, 2, frames + 2, 0, marks)
    build(xh, colh, act, edge, terms2, 0, 2, 1, marks)

    def stores(t):
        return [
            pltpu.make_async_copy(stage.at[t], out_hbm.at[t, :, k], out_sem.at[t, k]) for k in range(2)
        ]

    for t in range(frames):
        y = conv_frame(act, w2, t) + bias_ref[...]
        y = y + xl[t + 2, 1 : rows + 1].reshape(rows * cols, -1).astype(F32)
        for half in range(2):
            part = y[:, 128 * half : 128 * half + 128]
            wide[t % 2, half, pl.ds(0, rows * cols, stride=2), :] = part
            wide[t % 2, half, pl.ds(1, rows * cols, stride=2), :] = part
        for half in range(2):
            stage[t, :, :, 128 * half : 128 * half + 128] = (
                wide[t % 2, half].astype(BF16).reshape(rows, 2 * cols, 128)
            )
        for copy in stores(t):
            copy.start()
    for t in range(frames):
        for copy in stores(t):
            copy.wait()


def on_device(sizes, latent, gain_first, bias_first, kernel_first, gain_second, bias_second, kernel_second, conv_bias):
    n_tm, n_row, n_col = sizes
    frames, rows, cols, channels = latent.shape
    plane = n_row * n_col
    per_span = float(frames * rows * n_row * cols * n_col * (channels // GROUPS))
    tile = (frames + 2, rows + 2, cols, channels)
    tall = -(-(rows + 2) // 8) * 8
    cells = (2, frames + 2, tall, channels)
    send = (2, frames, tall, channels)
    taps = (27, channels, channels)
    anywhere = pl.BlockSpec(memory_space=pltpu.HBM)
    inside = pl.BlockSpec(memory_space=pltpu.VMEM)
    kept = [
        pltpu.VMEM(tile, BF16),
        pltpu.VMEM(tile, BF16),
        pltpu.VMEM(cells, BF16),
        pltpu.VMEM(taps, BF16),
        pltpu.VMEM((8, channels), F32),
    ]
    held = pl.pallas_call(
        functools.partial(first_kernel, sizes, per_span),
        out_shape=kept,
        in_specs=[anywhere] * 7,
        out_specs=[inside] * 5,
        scratch_shapes=[
            pltpu.VMEM((3, *tile), BF16),
            pltpu.VMEM(taps, BF16),
            pltpu.VMEM(cells, BF16),
            pltpu.VMEM(send, BF16),
            pltpu.VMEM(send, BF16),
            pltpu.VMEM((2, tall, channels), F32),
            pltpu.VMEM((tall, channels), F32),
            pltpu.VMEM((4, 1, channels), F32),
            pltpu.VMEM((8, channels), F32),
            pltpu.VMEM((2, 1, 128), F32),
            pltpu.VMEM((2, plane - 1, 1, 128), F32),
            pltpu.VMEM((2, 1, 128), F32),
            pltpu.VMEM((2, n_tm - 1, 1, 128), F32),
            pltpu.SemaphoreType.DMA((7,)),
            pltpu.SemaphoreType.DMA((N_COPIES,)),
            pltpu.SemaphoreType.DMA((N_COPIES,)),
            pltpu.SemaphoreType.DMA((4,)),
            pltpu.SemaphoreType.DMA((4,)),
        ],
        compiler_params=pltpu.CompilerParams(
            collective_id=0, has_side_effects=True, vmem_limit_bytes=24 * 2**20
        ),
        name="first_conv",
    )(
        *(
            pltpu.with_memory_space_constraint(x, pltpu.HBM)
            for x in (
                latent,
                kernel_first.reshape(taps),
                kernel_second.reshape(taps),
                gain_first.reshape(1, channels),
                bias_first.reshape(1, channels),
                gain_second.reshape(1, channels),
                bias_second.reshape(1, channels),
            )
        )
    )
    out = pl.pallas_call(
        functools.partial(second_kernel, sizes),
        out_shape=jax.ShapeDtypeStruct((frames, rows, 2, 2 * cols, channels), BF16),
        in_specs=[inside] * 6,
        out_specs=anywhere,
        scratch_shapes=[
            pltpu.VMEM((3, *tile), BF16),
            pltpu.VMEM((2, tall, channels), F32),
            pltpu.VMEM((2, 2, 2 * rows * cols, 128), F32),
            pltpu.VMEM((frames, rows, 2 * cols, channels), BF16),
            pltpu.SemaphoreType.DMA((frames, 2)),
        ],
        compiler_params=pltpu.CompilerParams(vmem_limit_bytes=24 * 2**20),
        name="second_conv",
    )(*held, conv_bias.reshape(1, channels))
    return out.reshape(frames, 2 * rows, 2 * cols, channels)


def solution(mesh):
    sizes = (mesh.shape["tm"], mesh.shape["row"], mesh.shape["col"])
    return jax.shard_map(
        functools.partial(on_device, sizes),
        mesh=mesh,
        in_specs=(P("tm", "row", "col", None), P(), P(), P(), P(), P(), P(), P()),
        out_specs=P("tm", "row", "col", None),
        check_vma=False,
    )
```

```python
import functools

import jax
import jax.numpy as jnp
from jax import lax
from jax.experimental import pallas as pl
from jax.experimental.pallas import tpu as pltpu
from jax.sharding import PartitionSpec as P

GROUPS = 32
EPSILON = 1e-06
MESH = pl.DeviceIdType.MESH
F32 = jnp.float32
BF16 = jnp.bfloat16


def lane_of(shape):
    return lax.broadcasted_iota(jnp.int32, shape, 1) % 8


def group_total(x):
    lane = lane_of(x.shape)
    lanes = x.shape[1]
    for step in (1, 2, 4):
        above = pltpu.roll(x, lanes - step, 1)
        below = pltpu.roll(x, step, 1)
        x = x + jnp.where((lane // step) % 2 == 0, above, below)
    return x


def pack_moments(total, square):
    rows = jnp.concatenate([total[:, :128], total[:, 128:], square[:, :128], square[:, 128:]], axis=0)
    rows = group_total(rows)
    lane = lane_of((1, 128))
    row = jnp.zeros((1, 128), F32)
    for k in range(4):
        row = jnp.where(lane == k, rows[k : k + 1], row)
    return row


def unpack_moments(row):
    lane = lane_of((1, 128))
    rows = jnp.concatenate([jnp.where(lane == k, row, 0.0) for k in range(4)], axis=0)
    rows = group_total(rows)
    total = jnp.concatenate([rows[0:1], rows[1:2]], axis=1)
    square = jnp.concatenate([rows[2:3], rows[3:4]], axis=1)
    return total, square


def half_terms(row, count, gain, bias):
    total, square = unpack_moments(row)
    mean = total / count
    scale = lax.rsqrt(square / count - mean * mean + EPSILON) * gain
    return 0.5 * scale, 0.5 * (bias - mean * scale)


def silu_of(x, scale, offset):
    u = x * scale + offset
    return u + u * jnp.tanh(u)


def build(x_ref, col_ref, act_ref, edge_ref, terms_ref, first, last, before, marks):
    north, south, west, east = marks
    rows = x_ref.shape[1]
    cols = x_ref.shape[2]
    scale = terms_ref[2 * before : 2 * before + 1, :]
    offset = terms_ref[2 * before + 1 : 2 * before + 2, :]
    at = lax.broadcasted_iota(jnp.int32, (col_ref.shape[2], 1), 0)
    inside = jnp.where(at == 0, north, jnp.where(at == rows - 1, south, 1.0))
    place = lax.broadcasted_iota(jnp.int32, (cols, 1), 0)

    @pl.loop(first, last)
    def _(t):
        for side, mark in ((0, west), (1, east)):
            keep = inside * mark
            edge_ref[side] = silu_of(col_ref[side, t].astype(F32), scale * keep, offset * keep)
        for h in range(rows):
            keep = north if h == 0 else south if h == rows - 1 else None
            s, o = (scale, offset) if keep is None else (scale * keep, offset * keep)
            z = silu_of(x_ref[t, h].astype(F32), s, o)
            act_ref[1, t, h] = z.astype(BF16)
            left = jnp.where(place == 0, edge_ref[0, h : h + 1, :], pltpu.roll(z, 1, 0))
            act_ref[0, t, h] = left.astype(BF16)
            right = jnp.where(place == cols - 1, edge_ref[1, h : h + 1, :], pltpu.roll(z, cols - 1, 0))
            act_ref[2, t, h] = right.astype(BF16)


def conv_frame(act_ref, w_ref, t):
    _, _, rows, cols, channels = act_ref.shape
    rows = rows - 2
    out = jnp.zeros((rows * cols, w_ref.shape[-1]), F32)
    for a in range(3):
        for b in range(3):
            for e in range(3):
                x = act_ref[e, t + a, b : b + rows].reshape(rows * cols, channels)
                out = out + jnp.dot(x, w_ref[(a * 3 + b) * 3 + e], preferred_element_type=F32)
    return out


def sums_of(x):
    parts = x.reshape(-1, 8, x.shape[-1])
    return jnp.sum(parts, axis=0), jnp.sum(parts * parts, axis=0)


def marks_of(n_row, n_col):
    row, col = lax.axis_index("row"), lax.axis_index("col")
    one, zero = jnp.float32(1.0), jnp.float32(0.0)
    return (
        jnp.where(row == 0, zero, one),
        jnp.where(row == n_row - 1, zero, one),
        jnp.where(col == 0, zero, one),
        jnp.where(col == n_col - 1, zero, one),
    )


def first_kernel(
    sizes, count,
    lat_hbm, w1_hbm, w2_hbm, gain1_hbm, bias1_hbm, gain2_hbm, bias2_hbm,
    xl, xh, colh, w2, terms2,
    act, w1, coll, send_l, send_h, edge, pick, affine, terms1,
    sum_send, plane_in, tm_send, tm_in,
    load_sem, send_sem, recv_sem, sum_send_sem, sum_recv_sem,
):
    n_tm, n_row, n_col = sizes
    tm, row, col = lax.axis_index("tm"), lax.axis_index("row"), lax.axis_index("col")
    frames, rows, cols = xl.shape[0] - 2, xl.shape[1] - 2, xl.shape[2]
    plane = n_row * n_col
    mine = row * n_col + col
    marks = marks_of(n_row, n_col)

    loads = [
        pltpu.make_async_copy(lat_hbm, xl.at[2:, 1 : rows + 1], load_sem.at[0]),
        pltpu.make_async_copy(gain1_hbm, affine.at[0], load_sem.at[1]),
        pltpu.make_async_copy(bias1_hbm, affine.at[1], load_sem.at[2]),
        pltpu.make_async_copy(gain2_hbm, affine.at[2], load_sem.at[3]),
        pltpu.make_async_copy(bias2_hbm, affine.at[3], load_sem.at[4]),
        pltpu.make_async_copy(w1_hbm, w1, load_sem.at[5]),
        pltpu.make_async_copy(w2_hbm, w2, load_sem.at[6]),
    ]
    for load in loads[:5]:
        load.start()

    def plane_peer(d):
        at = lax.rem(mine + d, plane)
        return (tm, at // n_col, lax.rem(at, n_col))

    def tm_peer(d):
        return (lax.rem(tm + d, n_tm), row, col)

    barrier = pltpu.get_barrier_semaphore()

    @pl.loop(1, plane)
    def _(d):
        pl.semaphore_signal(barrier, inc=1, device_id=plane_peer(d), device_id_type=MESH)

    @pl.loop(1, n_tm)
    def _(d):
        pl.semaphore_signal(barrier, inc=1, device_id=tm_peer(d), device_id_type=MESH)

    pick[...] = jnp.zeros_like(pick)
    north = (tm, lax.rem(row + n_row - 1, n_row), col)
    south = (tm, lax.rem(row + 1, n_row), col)
    west = (tm, row, lax.rem(col + n_col - 1, n_col))
    east = (tm, row, lax.rem(col + 1, n_col))
    later = tm_peer(1)

    def remote(src, dst, which, device):
        copy = pltpu.make_async_remote_copy(
            src_ref=src, dst_ref=dst, send_sem=send_sem.at[which], recv_sem=recv_sem.at[which],
            device_id=device, device_id_type=MESH,
        )
        copy.start()
        return copy

    def send_plane(which, moments):
        sum_send[which] = moments

        @pl.loop(1, plane)
        def _(d):
            pltpu.make_async_remote_copy(
                src_ref=sum_send.at[which], dst_ref=plane_in.at[which, d - 1],
                send_sem=sum_send_sem.at[which], recv_sem=sum_recv_sem.at[which],
                device_id=plane_peer(d), device_id_type=MESH,
            ).start()

    def all_plane(which, terms):
        pltpu.make_async_copy(plane_in.at[which], plane_in.at[which], sum_recv_sem.at[which]).wait()
        both = sum_send[which] + jnp.sum(plane_in[which], axis=0)
        done = tm.astype(F32)
        gain, bias = affine[2 * which], affine[2 * which + 1]
        scale, offset = half_terms(both, (done + 1.0) * count, gain, bias)
        terms[0:1, :] = scale
        terms[1:2, :] = offset
        prior = pltpu.roll(both, 124, 1)
        scale, offset = half_terms(prior, jnp.maximum(done, 1.0) * count, gain, bias)
        keep = jnp.where(tm == 0, jnp.float32(0.0), jnp.float32(1.0))
        terms[2:3, :] = scale * keep
        terms[3:4, :] = offset * keep

    def send_tm(which, moments):
        tm_send[which] = moments

        @pl.loop(1, n_tm)
        def _(d):
            pltpu.make_async_remote_copy(
                src_ref=tm_send.at[which], dst_ref=tm_in.at[which, d - 1],
                send_sem=sum_send_sem.at[2 + which], recv_sem=sum_recv_sem.at[2 + which],
                device_id=tm_peer(d), device_id_type=MESH,
            ).start()

    def all_tm(which):
        pltpu.make_async_copy(tm_in.at[which], tm_in.at[which], sum_recv_sem.at[2 + which]).wait()
        prior = jnp.zeros((1, 128), F32)
        for d in range(1, n_tm):
            prior = prior + jnp.where(tm >= d, tm_in[which, d - 1], 0.0)
        return prior + tm_send[which] + pltpu.roll(prior, 4, 1)

    def sums_sent(which):
        pltpu.make_async_copy(plane_in.at[which], plane_in.at[which], sum_send_sem.at[which]).wait()
        pltpu.make_async_copy(tm_in.at[which], tm_in.at[which], sum_send_sem.at[2 + which]).wait()

    def columns(x, out):
        for side, lo, at in ((0, cols - 8, 7), (1, 0, 0)):
            @pl.loop(2, frames + 2)
            def _(t):
                for h in range(rows + 2):
                    tile = x[t, h, lo : lo + 8, :].astype(F32)
                    pick[h : h + 1, :] = tile[at : at + 1, :]
                out[side, t - 2] = pick[...].astype(BF16)

    def halo_rows(x, base, lo, hi):
        return [
            remote(x.at[lo:hi, 1], x.at[lo:hi, rows + 1], base, north),
            remote(x.at[lo:hi, rows], x.at[lo:hi, 0], base + 1, south),
        ]

    def halo_columns(out, cells, base):
        return [
            remote(out.at[0], cells.at[0, 2:], base, east),
            remote(out.at[1], cells.at[1, 2:], base + 1, west),
        ]

    def onward_rows(x, base):
        return [
            remote(x.at[frames : frames + 2, 0], x.at[0:2, 0], base, later),
            remote(x.at[frames : frames + 2, rows + 1], x.at[0:2, rows + 1], base + 1, later),
        ]

    def onward_columns(cells, base):
        return [
            remote(cells.at[0, frames : frames + 2], cells.at[0, 0:2], base, later),
            remote(cells.at[1, frames : frames + 2], cells.at[1, 0:2], base + 1, later),
        ]

    def onward_frames(x, which, lo, hi):
        return [remote(x.at[frames + lo : frames + hi, 1 : rows + 1], x.at[lo:hi, 1 : rows + 1], which, later)]

    loads[0].wait()
    for load in loads[5:]:
        load.start()

    def add_frame(t, so_far):
        s, q = sums_of(xl[t, 1 : rows + 1].reshape(rows * cols, -1).astype(F32))
        return so_far[0] + s, so_far[1] + q

    none = jnp.zeros((8, xl.shape[-1]), F32)
    s, q = lax.fori_loop(2, frames + 2, add_frame, (none, none))
    moments = pack_moments(jnp.sum(s, axis=0, keepdims=True), jnp.sum(q, axis=0, keepdims=True))
    pl.semaphore_wait(barrier, plane - 1 + n_tm - 1)

    send_tm(0, moments)
    by_row = halo_rows(xl, 0, 2, frames + 2)
    onward = onward_frames(xl, 2, 0, 2)
    for copy in by_row:
        copy.wait_recv()
    columns(xl, send_l)
    by_col = halo_columns(send_l, coll, 3)
    onward += onward_rows(xl, 5)
    send_plane(0, all_tm(0))
    for copy in by_col:
        copy.wait_recv()
    onward += onward_columns(coll, 7)
    for load in loads[1:5]:
        load.wait()
    all_plane(0, terms1)

    build(xl, coll, act, edge, terms1, 2, frames + 2, 0, marks)
    loads[5].wait()

    def hidden_frame(t, so_far):
        h = conv_frame(act, w1, t).astype(BF16)
        xh[t + 2, 1 : rows + 1] = h.reshape(rows, cols, -1)
        s, q = sums_of(h.astype(F32))
        return so_far[0] + s, so_far[1] + q

    sums = hidden_frame(frames - 2, (none, none))
    onward2 = onward_frames(xh, 9, 0, 1)
    sums = hidden_frame(frames - 1, sums)
    by_row2 = halo_rows(xh, 10, frames, frames + 2)
    for copy in onward:
        copy.wait_recv()
    build(xl, coll, act, edge, terms1, 0, 2, 1, marks)
    s, q = lax.fori_loop(0, frames - 2, hidden_frame, sums)
    moments = pack_moments(jnp.sum(s, axis=0, keepdims=True), jnp.sum(q, axis=0, keepdims=True))
    send_tm(1, moments)
    onward2 += onward_frames(xh, 20, 1, 2)
    by_row2 += halo_rows(xh, 12, 2, frames)
    for copy in by_row2:
        copy.wait_recv()
    columns(xh, send_h)
    by_col2 = halo_columns(send_h, colh, 14)
    onward2 += onward_rows(xh, 16)
    send_plane(1, all_tm(1))
    for copy in by_col2:
        copy.wait_recv()
    onward2 += onward_columns(colh, 18)
    all_plane(1, terms2)
    loads[6].wait()
    for copy in onward2:
        copy.wait_recv()
    for copy in by_row + by_col + onward + by_row2 + by_col2 + onward2:
        copy.wait_send()
    sums_sent(0)
    sums_sent(1)


N_COPIES = 21


def second_kernel(
    sizes, xl, xh, colh, w2, terms2, bias_ref, out_hbm, act, edge, wide, stage, out_sem
):
    n_tm, n_row, n_col = sizes
    marks = marks_of(n_row, n_col)
    frames, rows, cols = xl.shape[0] - 2, xl.shape[1] - 2, xl.shape[2]
    build(xh, colh, act, edge, terms2, 2, frames + 2, 0, marks)
    build(xh, colh, act, edge, terms2, 0, 2, 1, marks)

    def stores(t):
        return [
            pltpu.make_async_copy(stage.at[t], out_hbm.at[t, :, k], out_sem.at[t, k]) for k in range(2)
        ]

    for t in range(frames):
        y = conv_frame(act, w2, t) + bias_ref[...]
        y = y + xl[t + 2, 1 : rows + 1].reshape(rows * cols, -1).astype(F32)
        for half in range(2):
            part = y[:, 128 * half : 128 * half + 128]
            wide[t % 2, half, pl.ds(0, rows * cols, stride=2), :] = part
            wide[t % 2, half, pl.ds(1, rows * cols, stride=2), :] = part
        for half in range(2):
            stage[t, :, :, 128 * half : 128 * half + 128] = (
                wide[t % 2, half].astype(BF16).reshape(rows, 2 * cols, 128)
            )
        for copy in stores(t):
            copy.start()
    for t in range(frames):
        for copy in stores(t):
            copy.wait()


def on_device(sizes, latent, gain_first, bias_first, kernel_first, gain_second, bias_second, kernel_second, conv_bias):
    n_tm, n_row, n_col = sizes
    frames, rows, cols, channels = latent.shape
    plane = n_row * n_col
    per_span = float(frames * rows * n_row * cols * n_col * (channels // GROUPS))
    tile = (frames + 2, rows + 2, cols, channels)
    tall = -(-(rows + 2) // 8) * 8
    cells = (2, frames + 2, tall, channels)
    send = (2, frames, tall, channels)
    taps = (27, channels, channels)
    anywhere = pl.BlockSpec(memory_space=pltpu.HBM)
    inside = pl.BlockSpec(memory_space=pltpu.VMEM)
    kept = [
        pltpu.VMEM(tile, BF16),
        pltpu.VMEM(tile, BF16),
        pltpu.VMEM(cells, BF16),
        pltpu.VMEM(taps, BF16),
        pltpu.VMEM((8, channels), F32),
    ]
    held = pl.pallas_call(
        functools.partial(first_kernel, sizes, per_span),
        out_shape=kept,
        in_specs=[anywhere] * 7,
        out_specs=[inside] * 5,
        scratch_shapes=[
            pltpu.VMEM((3, *tile), BF16),
            pltpu.VMEM(taps, BF16),
            pltpu.VMEM(cells, BF16),
            pltpu.VMEM(send, BF16),
            pltpu.VMEM(send, BF16),
            pltpu.VMEM((2, tall, channels), F32),
            pltpu.VMEM((tall, channels), F32),
            pltpu.VMEM((4, 1, channels), F32),
            pltpu.VMEM((8, channels), F32),
            pltpu.VMEM((2, 1, 128), F32),
            pltpu.VMEM((2, plane - 1, 1, 128), F32),
            pltpu.VMEM((2, 1, 128), F32),
            pltpu.VMEM((2, n_tm - 1, 1, 128), F32),
            pltpu.SemaphoreType.DMA((7,)),
            pltpu.SemaphoreType.DMA((N_COPIES,)),
            pltpu.SemaphoreType.DMA((N_COPIES,)),
            pltpu.SemaphoreType.DMA((4,)),
            pltpu.SemaphoreType.DMA((4,)),
        ],
        compiler_params=pltpu.CompilerParams(
            collective_id=0, has_side_effects=True, vmem_limit_bytes=24 * 2**20
        ),
        name="first_conv",
    )(
        *(
            pltpu.with_memory_space_constraint(x, pltpu.HBM)
            for x in (
                latent,
                kernel_first.reshape(taps),
                kernel_second.reshape(taps),
                gain_first.reshape(1, channels),
                bias_first.reshape(1, channels),
                gain_second.reshape(1, channels),
                bias_second.reshape(1, channels),
            )
        )
    )
    out = pl.pallas_call(
        functools.partial(second_kernel, sizes),
        out_shape=jax.ShapeDtypeStruct((frames, rows, 2, 2 * cols, channels), BF16),
        in_specs=[inside] * 6,
        out_specs=anywhere,
        scratch_shapes=[
            pltpu.VMEM((3, *tile), BF16),
            pltpu.VMEM((2, tall, channels), F32),
            pltpu.VMEM((2, 2, 2 * rows * cols, 128), F32),
            pltpu.VMEM((frames, rows, 2 * cols, channels), BF16),
            pltpu.SemaphoreType.DMA((frames, 2)),
        ],
        compiler_params=pltpu.CompilerParams(vmem_limit_bytes=24 * 2**20),
        name="second_conv",
    )(*held, conv_bias.reshape(1, channels))
    return out.reshape(frames, 2 * rows, 2 * cols, channels)


def solution(mesh):
    sizes = (mesh.shape["tm"], mesh.shape["row"], mesh.shape["col"])
    return jax.shard_map(
        functools.partial(on_device, sizes),
        mesh=mesh,
        in_specs=(P("tm", "row", "col", None), P(), P(), P(), P(), P(), P(), P()),
        out_specs=P("tm", "row", "col", None),
        check_vma=False,
    )
```

```python
import functools

import jax
import jax.numpy as jnp
from jax import lax
from jax.experimental import pallas as pl
from jax.experimental.pallas import tpu as pltpu
from jax.sharding import PartitionSpec as P

GROUPS = 32
EPSILON = 1e-06
MESH = pl.DeviceIdType.MESH
F32 = jnp.float32
BF16 = jnp.bfloat16


def lane_of(shape):
    return lax.broadcasted_iota(jnp.int32, shape, 1) % 8


def group_total(x):
    lane = lane_of(x.shape)
    lanes = x.shape[1]
    for step in (1, 2, 4):
        above = pltpu.roll(x, lanes - step, 1)
        below = pltpu.roll(x, step, 1)
        x = x + jnp.where((lane // step) % 2 == 0, above, below)
    return x


def pack_moments(total, square):
    rows = jnp.concatenate([total[:, :128], total[:, 128:], square[:, :128], square[:, 128:]], axis=0)
    rows = group_total(rows)
    lane = lane_of((1, 128))
    row = jnp.zeros((1, 128), F32)
    for k in range(4):
        row = jnp.where(lane == k, rows[k : k + 1], row)
    return row


def unpack_moments(row):
    lane = lane_of((1, 128))
    rows = jnp.concatenate([jnp.where(lane == k, row, 0.0) for k in range(4)], axis=0)
    rows = group_total(rows)
    total = jnp.concatenate([rows[0:1], rows[1:2]], axis=1)
    square = jnp.concatenate([rows[2:3], rows[3:4]], axis=1)
    return total, square


def half_terms(row, count, gain, bias):
    total, square = unpack_moments(row)
    mean = total / count
    scale = lax.rsqrt(square / count - mean * mean + EPSILON) * gain
    return 0.5 * scale, 0.5 * (bias - mean * scale)


def silu_of(x, scale, offset):
    u = x * scale + offset
    return u + u * jnp.tanh(u)


def build(x_ref, col_ref, act_ref, edge_ref, terms_ref, first, last, before, marks):
    north, south, west, east = marks
    rows = x_ref.shape[1]
    cols = x_ref.shape[2]
    scale = terms_ref[2 * before : 2 * before + 1, :]
    offset = terms_ref[2 * before + 1 : 2 * before + 2, :]
    at = lax.broadcasted_iota(jnp.int32, (col_ref.shape[2], 1), 0)
    inside = jnp.where(at == 0, north, jnp.where(at == rows - 1, south, 1.0))
    place = lax.broadcasted_iota(jnp.int32, (cols, 1), 0)

    @pl.loop(first, last)
    def _(t):
        for side, mark in ((0, west), (1, east)):
            keep = inside * mark
            edge_ref[side] = silu_of(col_ref[side, t].astype(F32), scale * keep, offset * keep)
        for h in range(rows):
            keep = north if h == 0 else south if h == rows - 1 else None
            s, o = (scale, offset) if keep is None else (scale * keep, offset * keep)
            z = silu_of(x_ref[t, h].astype(F32), s, o)
            act_ref[1, t, h] = z.astype(BF16)
            left = jnp.where(place == 0, edge_ref[0, h : h + 1, :], pltpu.roll(z, 1, 0))
            act_ref[0, t, h] = left.astype(BF16)
            right = jnp.where(place == cols - 1, edge_ref[1, h : h + 1, :], pltpu.roll(z, cols - 1, 0))
            act_ref[2, t, h] = right.astype(BF16)


def conv_frame(act_ref, w_ref, t):
    _, _, rows, cols, channels = act_ref.shape
    rows = rows - 2
    out = jnp.zeros((rows * cols, w_ref.shape[-1]), F32)
    for a in range(3):
        for b in range(3):
            for e in range(3):
                x = act_ref[e, t + a, b : b + rows].reshape(rows * cols, channels)
                out = out + jnp.dot(x, w_ref[(a * 3 + b) * 3 + e], preferred_element_type=F32)
    return out


def sums_of(x):
    parts = x.reshape(-1, 8, x.shape[-1])
    return jnp.sum(parts, axis=0), jnp.sum(parts * parts, axis=0)


def marks_of(n_row, n_col):
    row, col = lax.axis_index("row"), lax.axis_index("col")
    one, zero = jnp.float32(1.0), jnp.float32(0.0)
    return (
        jnp.where(row == 0, zero, one),
        jnp.where(row == n_row - 1, zero, one),
        jnp.where(col == 0, zero, one),
        jnp.where(col == n_col - 1, zero, one),
    )


def first_kernel(
    sizes, count,
    lat_hbm, w1_hbm, w2_hbm, gain1_hbm, bias1_hbm, gain2_hbm, bias2_hbm,
    xl, xh, colh, w2, terms2,
    act, w1, coll, send_l, send_h, edge, pick, affine, terms1,
    tm_send, tm_in, col_send, col_in, row_send, row_in,
    load_sem, send_sem, recv_sem, sum_send_sem, sum_recv_sem,
):
    n_tm, n_row, n_col = sizes
    tm, row, col = lax.axis_index("tm"), lax.axis_index("row"), lax.axis_index("col")
    frames, rows, cols = xl.shape[0] - 2, xl.shape[1] - 2, xl.shape[2]
    marks = marks_of(n_row, n_col)

    loads = [
        pltpu.make_async_copy(lat_hbm, xl.at[2:, 1 : rows + 1], load_sem.at[0]),
        pltpu.make_async_copy(gain1_hbm, affine.at[0], load_sem.at[1]),
        pltpu.make_async_copy(bias1_hbm, affine.at[1], load_sem.at[2]),
        pltpu.make_async_copy(gain2_hbm, affine.at[2], load_sem.at[3]),
        pltpu.make_async_copy(bias2_hbm, affine.at[3], load_sem.at[4]),
        pltpu.make_async_copy(w1_hbm, w1, load_sem.at[5]),
        pltpu.make_async_copy(w2_hbm, w2, load_sem.at[6]),
    ]
    for load in loads[:5]:
        load.start()

    def tm_peer(d):
        return (lax.rem(tm + d, n_tm), row, col)

    def col_peer(d):
        return (tm, row, lax.rem(col + d, n_col))

    def row_peer(d):
        return (tm, lax.rem(row + d, n_row), col)

    TM, COL, ROW = 0, 1, 2
    exchanges = (
        (n_tm, tm_peer, tm_send, tm_in),
        (n_col, col_peer, col_send, col_in),
        (n_row, row_peer, row_send, row_in),
    )

    barrier = pltpu.get_barrier_semaphore()
    for n, peer, _, _ in exchanges:
        for d in range(1, n):
            pl.semaphore_signal(barrier, inc=1, device_id=peer(d), device_id_type=MESH)

    pick[...] = jnp.zeros_like(pick)
    north = (tm, lax.rem(row + n_row - 1, n_row), col)
    south = (tm, lax.rem(row + 1, n_row), col)
    west = (tm, row, lax.rem(col + n_col - 1, n_col))
    east = (tm, row, lax.rem(col + 1, n_col))
    later = tm_peer(1)

    def remote(src, dst, which, device):
        copy = pltpu.make_async_remote_copy(
            src_ref=src, dst_ref=dst, send_sem=send_sem.at[which], recv_sem=recv_sem.at[which],
            device_id=device, device_id_type=MESH,
        )
        copy.start()
        return copy

    def send_sums(stage, which, sums):
        n, peer, held, arrived = exchanges[stage]
        held[which] = sums
        for d in sorted(range(1, n), key=lambda d: -min(d, n - d)):
            pltpu.make_async_remote_copy(
                src_ref=held.at[which], dst_ref=arrived.at[which, d - 1],
                send_sem=sum_send_sem.at[2 * stage + which], recv_sem=sum_recv_sem.at[2 * stage + which],
                device_id=peer(d), device_id_type=MESH,
            ).start()

    def wait_sums(stage, which):
        arrived = exchanges[stage][3].at[which]
        pltpu.make_async_copy(arrived, arrived, sum_recv_sem.at[2 * stage + which]).wait()

    def all_along(stage, which):
        wait_sums(stage, which)
        held, arrived = exchanges[stage][2:]
        return held[which] + jnp.sum(arrived[which], axis=0)

    def all_terms(which, terms):
        both = all_along(ROW, which)
        done = tm.astype(F32)
        gain, bias = affine[2 * which], affine[2 * which + 1]
        scale, offset = half_terms(both, (done + 1.0) * count, gain, bias)
        terms[0:1, :] = scale
        terms[1:2, :] = offset
        prior = pltpu.roll(both, 124, 1)
        scale, offset = half_terms(prior, jnp.maximum(done, 1.0) * count, gain, bias)
        keep = jnp.where(tm == 0, jnp.float32(0.0), jnp.float32(1.0))
        terms[2:3, :] = scale * keep
        terms[3:4, :] = offset * keep

    def all_tm(which):
        wait_sums(TM, which)
        prior = jnp.zeros((1, 128), F32)
        for d in range(1, n_tm):
            prior = prior + jnp.where(tm >= d, tm_in[which, d - 1], 0.0)
        return prior + tm_send[which] + pltpu.roll(prior, 4, 1)

    def sums_sent(which):
        for stage in (TM, COL, ROW):
            arrived = exchanges[stage][3].at[which]
            pltpu.make_async_copy(arrived, arrived, sum_send_sem.at[2 * stage + which]).wait()

    def columns(x, out):
        for side, lo, at in ((0, cols - 8, 7), (1, 0, 0)):
            @pl.loop(2, frames + 2)
            def _(t):
                for h in range(rows + 2):
                    tile = x[t, h, lo : lo + 8, :].astype(F32)
                    pick[h : h + 1, :] = tile[at : at + 1, :]
                out[side, t - 2] = pick[...].astype(BF16)

    def halo_rows(x, base, lo, hi):
        return [
            remote(x.at[lo:hi, 1], x.at[lo:hi, rows + 1], base, north),
            remote(x.at[lo:hi, rows], x.at[lo:hi, 0], base + 1, south),
        ]

    def halo_columns(out, cells, base):
        return [
            remote(out.at[0], cells.at[0, 2:], base, east),
            remote(out.at[1], cells.at[1, 2:], base + 1, west),
        ]

    def onward_rows(x, base):
        return [
            remote(x.at[frames : frames + 2, 0], x.at[0:2, 0], base, later),
            remote(x.at[frames : frames + 2, rows + 1], x.at[0:2, rows + 1], base + 1, later),
        ]

    def onward_columns(cells, base):
        return [
            remote(cells.at[0, frames : frames + 2], cells.at[0, 0:2], base, later),
            remote(cells.at[1, frames : frames + 2], cells.at[1, 0:2], base + 1, later),
        ]

    def onward_frames(x, which, lo, hi):
        return [remote(x.at[frames + lo : frames + hi, 1 : rows + 1], x.at[lo:hi, 1 : rows + 1], which, later)]

    loads[0].wait()
    for load in loads[5:]:
        load.start()

    def add_frame(t, so_far):
        s, q = sums_of(xl[t, 1 : rows + 1].reshape(rows * cols, -1).astype(F32))
        return so_far[0] + s, so_far[1] + q

    none = jnp.zeros((8, xl.shape[-1]), F32)
    s, q = lax.fori_loop(2, frames + 2, add_frame, (none, none))
    moments = pack_moments(jnp.sum(s, axis=0, keepdims=True), jnp.sum(q, axis=0, keepdims=True))
    pl.semaphore_wait(barrier, n_tm + n_col + n_row - 3)

    send_sums(TM, 0, moments)
    by_row = halo_rows(xl, 0, 2, frames + 2)
    onward = onward_frames(xl, 2, 0, 2)
    for copy in by_row:
        copy.wait_recv()
    columns(xl, send_l)
    by_col = halo_columns(send_l, coll, 3)
    onward += onward_rows(xl, 5)
    send_sums(COL, 0, all_tm(0))
    for copy in by_col:
        copy.wait_recv()
    onward += onward_columns(coll, 7)
    for load in loads[1:5]:
        load.wait()
    send_sums(ROW, 0, all_along(COL, 0))
    all_terms(0, terms1)

    build(xl, coll, act, edge, terms1, 2, frames + 2, 0, marks)
    loads[5].wait()

    def hidden_frame(t, so_far):
        h = conv_frame(act, w1, t).astype(BF16)
        xh[t + 2, 1 : rows + 1] = h.reshape(rows, cols, -1)
        s, q = sums_of(h.astype(F32))
        return so_far[0] + s, so_far[1] + q

    sums = hidden_frame(frames - 2, (none, none))
    onward2 = onward_frames(xh, 9, 0, 1)
    sums = hidden_frame(frames - 1, sums)
    by_row2 = halo_rows(xh, 10, frames, frames + 2)
    for copy in onward:
        copy.wait_recv()
    build(xl, coll, act, edge, terms1, 0, 2, 1, marks)
    s, q = lax.fori_loop(0, frames - 2, hidden_frame, sums)
    moments = pack_moments(jnp.sum(s, axis=0, keepdims=True), jnp.sum(q, axis=0, keepdims=True))
    send_sums(TM, 1, moments)
    onward2 += onward_frames(xh, 20, 1, 2)
    by_row2 += halo_rows(xh, 12, 2, frames)
    for copy in by_row2:
        copy.wait_recv()
    columns(xh, send_h)
    by_col2 = halo_columns(send_h, colh, 14)
    onward2 += onward_rows(xh, 16)
    send_sums(COL, 1, all_tm(1))
    for copy in by_col2:
        copy.wait_recv()
    onward2 += onward_columns(colh, 18)
    send_sums(ROW, 1, all_along(COL, 1))
    all_terms(1, terms2)
    loads[6].wait()
    for copy in onward2:
        copy.wait_recv()
    for copy in by_row + by_col + onward + by_row2 + by_col2 + onward2:
        copy.wait_send()
    sums_sent(0)
    sums_sent(1)


N_COPIES = 21


def second_kernel(
    sizes, xl, xh, colh, w2, terms2, bias_ref, out_hbm, act, edge, wide, stage, out_sem
):
    n_tm, n_row, n_col = sizes
    marks = marks_of(n_row, n_col)
    frames, rows, cols = xl.shape[0] - 2, xl.shape[1] - 2, xl.shape[2]
    build(xh, colh, act, edge, terms2, 2, frames + 2, 0, marks)
    build(xh, colh, act, edge, terms2, 0, 2, 1, marks)

    def stores(t):
        return [
            pltpu.make_async_copy(stage.at[t], out_hbm.at[t, :, k], out_sem.at[t, k]) for k in range(2)
        ]

    for t in range(frames):
        y = conv_frame(act, w2, t) + bias_ref[...]
        y = y + xl[t + 2, 1 : rows + 1].reshape(rows * cols, -1).astype(F32)
        for half in range(2):
            part = y[:, 128 * half : 128 * half + 128]
            wide[t % 2, half, pl.ds(0, rows * cols, stride=2), :] = part
            wide[t % 2, half, pl.ds(1, rows * cols, stride=2), :] = part
        for half in range(2):
            stage[t, :, :, 128 * half : 128 * half + 128] = (
                wide[t % 2, half].astype(BF16).reshape(rows, 2 * cols, 128)
            )
        for copy in stores(t):
            copy.start()
    for t in range(frames):
        for copy in stores(t):
            copy.wait()


def on_device(sizes, latent, gain_first, bias_first, kernel_first, gain_second, bias_second, kernel_second, conv_bias):
    n_tm, n_row, n_col = sizes
    frames, rows, cols, channels = latent.shape
    per_span = float(frames * rows * n_row * cols * n_col * (channels // GROUPS))
    tile = (frames + 2, rows + 2, cols, channels)
    tall = -(-(rows + 2) // 8) * 8
    cells = (2, frames + 2, tall, channels)
    send = (2, frames, tall, channels)
    taps = (27, channels, channels)
    anywhere = pl.BlockSpec(memory_space=pltpu.HBM)
    inside = pl.BlockSpec(memory_space=pltpu.VMEM)
    kept = [
        pltpu.VMEM(tile, BF16),
        pltpu.VMEM(tile, BF16),
        pltpu.VMEM(cells, BF16),
        pltpu.VMEM(taps, BF16),
        pltpu.VMEM((8, channels), F32),
    ]
    held = pl.pallas_call(
        functools.partial(first_kernel, sizes, per_span),
        out_shape=kept,
        in_specs=[anywhere] * 7,
        out_specs=[inside] * 5,
        scratch_shapes=[
            pltpu.VMEM((3, *tile), BF16),
            pltpu.VMEM(taps, BF16),
            pltpu.VMEM(cells, BF16),
            pltpu.VMEM(send, BF16),
            pltpu.VMEM(send, BF16),
            pltpu.VMEM((2, tall, channels), F32),
            pltpu.VMEM((tall, channels), F32),
            pltpu.VMEM((4, 1, channels), F32),
            pltpu.VMEM((8, channels), F32),
            pltpu.VMEM((2, 1, 128), F32),
            pltpu.VMEM((2, n_tm - 1, 1, 128), F32),
            pltpu.VMEM((2, 1, 128), F32),
            pltpu.VMEM((2, n_col - 1, 1, 128), F32),
            pltpu.VMEM((2, 1, 128), F32),
            pltpu.VMEM((2, n_row - 1, 1, 128), F32),
            pltpu.SemaphoreType.DMA((7,)),
            pltpu.SemaphoreType.DMA((N_COPIES,)),
            pltpu.SemaphoreType.DMA((N_COPIES,)),
            pltpu.SemaphoreType.DMA((6,)),
            pltpu.SemaphoreType.DMA((6,)),
        ],
        compiler_params=pltpu.CompilerParams(
            collective_id=0, has_side_effects=True, vmem_limit_bytes=24 * 2**20
        ),
        name="first_conv",
    )(
        *(
            pltpu.with_memory_space_constraint(x, pltpu.HBM)
            for x in (
                latent,
                kernel_first.reshape(taps),
                kernel_second.reshape(taps),
                gain_first.reshape(1, channels),
                bias_first.reshape(1, channels),
                gain_second.reshape(1, channels),
                bias_second.reshape(1, channels),
            )
        )
    )
    out = pl.pallas_call(
        functools.partial(second_kernel, sizes),
        out_shape=jax.ShapeDtypeStruct((frames, rows, 2, 2 * cols, channels), BF16),
        in_specs=[inside] * 6,
        out_specs=anywhere,
        scratch_shapes=[
            pltpu.VMEM((3, *tile), BF16),
            pltpu.VMEM((2, tall, channels), F32),
            pltpu.VMEM((2, 2, 2 * rows * cols, 128), F32),
            pltpu.VMEM((frames, rows, 2 * cols, channels), BF16),
            pltpu.SemaphoreType.DMA((frames, 2)),
        ],
        compiler_params=pltpu.CompilerParams(vmem_limit_bytes=24 * 2**20),
        name="second_conv",
    )(*held, conv_bias.reshape(1, channels))
    return out.reshape(frames, 2 * rows, 2 * cols, channels)


def solution(mesh):
    sizes = (mesh.shape["tm"], mesh.shape["row"], mesh.shape["col"])
    return jax.shard_map(
        functools.partial(on_device, sizes),
        mesh=mesh,
        in_specs=(P("tm", "row", "col", None), P(), P(), P(), P(), P(), P(), P()),
        out_specs=P("tm", "row", "col", None),
        check_vma=False,
    )
```

```python
import functools

import jax
import jax.numpy as jnp
from jax import lax
from jax.experimental import pallas as pl
from jax.experimental.pallas import tpu as pltpu
from jax.sharding import PartitionSpec as P

GROUPS = 32
EPSILON = 1e-06
MESH = pl.DeviceIdType.MESH
F32 = jnp.float32
BF16 = jnp.bfloat16


def lane_of(shape):
    return lax.broadcasted_iota(jnp.int32, shape, 1) % 8


def group_total(x):
    lane = lane_of(x.shape)
    lanes = x.shape[1]
    for step in (1, 2, 4):
        above = pltpu.roll(x, lanes - step, 1)
        below = pltpu.roll(x, step, 1)
        x = x + jnp.where((lane // step) % 2 == 0, above, below)
    return x


def pack_moments(total, square):
    rows = jnp.concatenate([total[:, :128], total[:, 128:], square[:, :128], square[:, 128:]], axis=0)
    rows = group_total(rows)
    lane = lane_of((1, 128))
    row = jnp.zeros((1, 128), F32)
    for k in range(4):
        row = jnp.where(lane == k, rows[k : k + 1], row)
    return row


def unpack_moments(row):
    lane = lane_of((1, 128))
    rows = jnp.concatenate([jnp.where(lane == k, row, 0.0) for k in range(4)], axis=0)
    rows = group_total(rows)
    total = jnp.concatenate([rows[0:1], rows[1:2]], axis=1)
    square = jnp.concatenate([rows[2:3], rows[3:4]], axis=1)
    return total, square


def half_terms(row, count, gain, bias):
    total, square = unpack_moments(row)
    mean = total / count
    scale = lax.rsqrt(square / count - mean * mean + EPSILON) * gain
    return 0.5 * scale, 0.5 * (bias - mean * scale)


def silu_of(x, scale, offset):
    u = x * scale + offset
    return u + u * jnp.tanh(u)


def build(x_ref, col_ref, act_ref, edge_ref, terms_ref, first, last, before, marks):
    north, south, west, east = marks
    rows = x_ref.shape[1]
    cols = x_ref.shape[2]
    scale = terms_ref[2 * before : 2 * before + 1, :]
    offset = terms_ref[2 * before + 1 : 2 * before + 2, :]
    at = lax.broadcasted_iota(jnp.int32, (col_ref.shape[2], 1), 0)
    inside = jnp.where(at == 0, north, jnp.where(at == rows - 1, south, 1.0))
    place = lax.broadcasted_iota(jnp.int32, (cols, 1), 0)

    @pl.loop(first, last)
    def _(t):
        for side, mark in ((0, west), (1, east)):
            keep = inside * mark
            edge_ref[side] = silu_of(col_ref[side, t].astype(F32), scale * keep, offset * keep)
        for h in range(rows):
            keep = north if h == 0 else south if h == rows - 1 else None
            s, o = (scale, offset) if keep is None else (scale * keep, offset * keep)
            z = silu_of(x_ref[t, h].astype(F32), s, o)
            act_ref[1, t, h] = z.astype(BF16)
            left = jnp.where(place == 0, edge_ref[0, h : h + 1, :], pltpu.roll(z, 1, 0))
            act_ref[0, t, h] = left.astype(BF16)
            right = jnp.where(place == cols - 1, edge_ref[1, h : h + 1, :], pltpu.roll(z, cols - 1, 0))
            act_ref[2, t, h] = right.astype(BF16)


def conv_frame(act_ref, w_ref, t):
    _, _, rows, cols, channels = act_ref.shape
    rows = rows - 2
    out = jnp.zeros((rows * cols, w_ref.shape[-1]), F32)
    for a in range(3):
        for b in range(3):
            for e in range(3):
                x = act_ref[e, t + a, b : b + rows].reshape(rows * cols, channels)
                out = out + jnp.dot(x, w_ref[(a * 3 + b) * 3 + e], preferred_element_type=F32)
    return out


def sums_of(x):
    parts = x.reshape(-1, 8, x.shape[-1])
    return jnp.sum(parts, axis=0), jnp.sum(parts * parts, axis=0)


def marks_of(n_row, n_col):
    row, col = lax.axis_index("row"), lax.axis_index("col")
    one, zero = jnp.float32(1.0), jnp.float32(0.0)
    return (
        jnp.where(row == 0, zero, one),
        jnp.where(row == n_row - 1, zero, one),
        jnp.where(col == 0, zero, one),
        jnp.where(col == n_col - 1, zero, one),
    )


def first_kernel(
    sizes, count,
    lat_hbm, w1_hbm, w2_hbm, gain1_hbm, bias1_hbm, gain2_hbm, bias2_hbm,
    xl, xh, colh, w2, terms2,
    act, w1, coll, send_l, send_h, edge, pick, affine, terms1,
    sum_send, plane_in, tm_send, tm_in,
    load_sem, send_sem, recv_sem, sum_send_sem, sum_recv_sem,
):
    n_tm, n_row, n_col = sizes
    tm, row, col = lax.axis_index("tm"), lax.axis_index("row"), lax.axis_index("col")
    frames, rows, cols = xl.shape[0] - 2, xl.shape[1] - 2, xl.shape[2]
    plane = n_row * n_col
    marks = marks_of(n_row, n_col)

    loads = [
        pltpu.make_async_copy(lat_hbm, xl.at[2:, 1 : rows + 1], load_sem.at[0]),
        pltpu.make_async_copy(gain1_hbm, affine.at[0], load_sem.at[1]),
        pltpu.make_async_copy(bias1_hbm, affine.at[1], load_sem.at[2]),
        pltpu.make_async_copy(gain2_hbm, affine.at[2], load_sem.at[3]),
        pltpu.make_async_copy(bias2_hbm, affine.at[3], load_sem.at[4]),
        pltpu.make_async_copy(w1_hbm, w1, load_sem.at[5]),
        pltpu.make_async_copy(w2_hbm, w2, load_sem.at[6]),
    ]
    for load in loads[:5]:
        load.start()

    def plane_peer(d):
        return (tm, lax.rem(row + d // n_col, n_row), lax.rem(col + d % n_col, n_col))

    def plane_hops(d):
        down, along = d // n_col, d % n_col
        return min(down, n_row - down) + min(along, n_col - along)

    def tm_peer(d):
        return (lax.rem(tm + d, n_tm), row, col)

    barrier = pltpu.get_barrier_semaphore()

    @pl.loop(1, plane)
    def _(d):
        pl.semaphore_signal(barrier, inc=1, device_id=plane_peer(d), device_id_type=MESH)

    @pl.loop(1, n_tm)
    def _(d):
        pl.semaphore_signal(barrier, inc=1, device_id=tm_peer(d), device_id_type=MESH)

    pick[...] = jnp.zeros_like(pick)
    north = (tm, lax.rem(row + n_row - 1, n_row), col)
    south = (tm, lax.rem(row + 1, n_row), col)
    west = (tm, row, lax.rem(col + n_col - 1, n_col))
    east = (tm, row, lax.rem(col + 1, n_col))
    later = tm_peer(1)

    def remote(src, dst, which, device):
        copy = pltpu.make_async_remote_copy(
            src_ref=src, dst_ref=dst, send_sem=send_sem.at[which], recv_sem=recv_sem.at[which],
            device_id=device, device_id_type=MESH,
        )
        copy.start()
        return copy

    def send_plane(which, moments):
        sum_send[which] = moments

        for d in sorted(range(1, plane), key=plane_hops, reverse=True):
            pltpu.make_async_remote_copy(
                src_ref=sum_send.at[which], dst_ref=plane_in.at[which, d - 1],
                send_sem=sum_send_sem.at[which], recv_sem=sum_recv_sem.at[which],
                device_id=plane_peer(d), device_id_type=MESH,
            ).start()

    def all_plane(which, terms):
        pltpu.make_async_copy(plane_in.at[which], plane_in.at[which], sum_recv_sem.at[which]).wait()
        both = sum_send[which] + jnp.sum(plane_in[which], axis=0)
        done = tm.astype(F32)
        gain, bias = affine[2 * which], affine[2 * which + 1]
        scale, offset = half_terms(both, (done + 1.0) * count, gain, bias)
        terms[0:1, :] = scale
        terms[1:2, :] = offset
        prior = pltpu.roll(both, 124, 1)
        scale, offset = half_terms(prior, jnp.maximum(done, 1.0) * count, gain, bias)
        keep = jnp.where(tm == 0, jnp.float32(0.0), jnp.float32(1.0))
        terms[2:3, :] = scale * keep
        terms[3:4, :] = offset * keep

    def send_tm(which, moments):
        tm_send[which] = moments

        for d in sorted(range(1, n_tm), key=lambda d: min(d, n_tm - d), reverse=True):
            pltpu.make_async_remote_copy(
                src_ref=tm_send.at[which], dst_ref=tm_in.at[which, d - 1],
                send_sem=sum_send_sem.at[2 + which], recv_sem=sum_recv_sem.at[2 + which],
                device_id=tm_peer(d), device_id_type=MESH,
            ).start()

    def all_tm(which):
        pltpu.make_async_copy(tm_in.at[which], tm_in.at[which], sum_recv_sem.at[2 + which]).wait()
        prior = jnp.zeros((1, 128), F32)
        for d in range(1, n_tm):
            prior = prior + jnp.where(tm >= d, tm_in[which, d - 1], 0.0)
        return prior + tm_send[which] + pltpu.roll(prior, 4, 1)

    def sums_sent(which):
        pltpu.make_async_copy(plane_in.at[which], plane_in.at[which], sum_send_sem.at[which]).wait()
        pltpu.make_async_copy(tm_in.at[which], tm_in.at[which], sum_send_sem.at[2 + which]).wait()

    def columns(x, out):
        for side, lo, at in ((0, cols - 8, 7), (1, 0, 0)):
            @pl.loop(2, frames + 2)
            def _(t):
                for h in range(rows + 2):
                    tile = x[t, h, lo : lo + 8, :].astype(F32)
                    pick[h : h + 1, :] = tile[at : at + 1, :]
                out[side, t - 2] = pick[...].astype(BF16)

    def halo_rows(x, base, lo, hi):
        return [
            remote(x.at[lo:hi, 1], x.at[lo:hi, rows + 1], base, north),
            remote(x.at[lo:hi, rows], x.at[lo:hi, 0], base + 1, south),
        ]

    def halo_columns(out, cells, base):
        return [
            remote(out.at[0], cells.at[0, 2:], base, east),
            remote(out.at[1], cells.at[1, 2:], base + 1, west),
        ]

    def onward_rows(x, base):
        return [
            remote(x.at[frames : frames + 2, 0], x.at[0:2, 0], base, later),
            remote(x.at[frames : frames + 2, rows + 1], x.at[0:2, rows + 1], base + 1, later),
        ]

    def onward_columns(cells, base):
        return [
            remote(cells.at[0, frames : frames + 2], cells.at[0, 0:2], base, later),
            remote(cells.at[1, frames : frames + 2], cells.at[1, 0:2], base + 1, later),
        ]

    def onward_frames(x, which, lo, hi):
        return [remote(x.at[frames + lo : frames + hi, 1 : rows + 1], x.at[lo:hi, 1 : rows + 1], which, later)]

    loads[0].wait()
    for load in loads[5:]:
        load.start()

    def add_frame(t, so_far):
        s, q = sums_of(xl[t, 1 : rows + 1].reshape(rows * cols, -1).astype(F32))
        return so_far[0] + s, so_far[1] + q

    none = jnp.zeros((8, xl.shape[-1]), F32)
    s, q = lax.fori_loop(2, frames + 2, add_frame, (none, none))
    moments = pack_moments(jnp.sum(s, axis=0, keepdims=True), jnp.sum(q, axis=0, keepdims=True))
    pl.semaphore_wait(barrier, plane - 1 + n_tm - 1)

    send_tm(0, moments)
    by_row = halo_rows(xl, 0, 2, frames + 2)
    onward = onward_frames(xl, 2, 0, 2)
    for copy in by_row:
        copy.wait_recv()
    columns(xl, send_l)
    by_col = halo_columns(send_l, coll, 3)
    onward += onward_rows(xl, 5)
    send_plane(0, all_tm(0))
    for copy in by_col:
        copy.wait_recv()
    onward += onward_columns(coll, 7)
    for load in loads[1:5]:
        load.wait()
    all_plane(0, terms1)

    build(xl, coll, act, edge, terms1, 2, frames + 2, 0, marks)
    loads[5].wait()

    def hidden_frame(t, so_far):
        h = conv_frame(act, w1, t).astype(BF16)
        xh[t + 2, 1 : rows + 1] = h.reshape(rows, cols, -1)
        s, q = sums_of(h.astype(F32))
        return so_far[0] + s, so_far[1] + q

    sums = hidden_frame(frames - 2, (none, none))
    onward2 = onward_frames(xh, 9, 0, 1)
    sums = hidden_frame(frames - 1, sums)
    by_row2 = halo_rows(xh, 10, frames, frames + 2)
    for copy in onward:
        copy.wait_recv()
    build(xl, coll, act, edge, terms1, 0, 2, 1, marks)
    s, q = lax.fori_loop(0, frames - 2, hidden_frame, sums)
    moments = pack_moments(jnp.sum(s, axis=0, keepdims=True), jnp.sum(q, axis=0, keepdims=True))
    send_tm(1, moments)
    onward2 += onward_frames(xh, 20, 1, 2)
    by_row2 += halo_rows(xh, 12, 2, frames)
    for copy in by_row2:
        copy.wait_recv()
    columns(xh, send_h)
    by_col2 = halo_columns(send_h, colh, 14)
    onward2 += onward_rows(xh, 16)
    send_plane(1, all_tm(1))
    for copy in by_col2:
        copy.wait_recv()
    onward2 += onward_columns(colh, 18)
    all_plane(1, terms2)
    loads[6].wait()
    for copy in onward2:
        copy.wait_recv()
    for copy in by_row + by_col + onward + by_row2 + by_col2 + onward2:
        copy.wait_send()
    sums_sent(0)
    sums_sent(1)


N_COPIES = 21


def second_kernel(
    sizes, xl, xh, colh, w2, terms2, bias_ref, out_hbm, act, edge, wide, stage, out_sem
):
    n_tm, n_row, n_col = sizes
    marks = marks_of(n_row, n_col)
    frames, rows, cols = xl.shape[0] - 2, xl.shape[1] - 2, xl.shape[2]
    build(xh, colh, act, edge, terms2, 2, frames + 2, 0, marks)
    build(xh, colh, act, edge, terms2, 0, 2, 1, marks)

    def stores(t):
        return [
            pltpu.make_async_copy(stage.at[t], out_hbm.at[t, :, k], out_sem.at[t, k]) for k in range(2)
        ]

    for t in range(frames):
        y = conv_frame(act, w2, t) + bias_ref[...]
        y = y + xl[t + 2, 1 : rows + 1].reshape(rows * cols, -1).astype(F32)
        for half in range(2):
            part = y[:, 128 * half : 128 * half + 128]
            wide[t % 2, half, pl.ds(0, rows * cols, stride=2), :] = part
            wide[t % 2, half, pl.ds(1, rows * cols, stride=2), :] = part
        for half in range(2):
            stage[t, :, :, 128 * half : 128 * half + 128] = (
                wide[t % 2, half].astype(BF16).reshape(rows, 2 * cols, 128)
            )
        for copy in stores(t):
            copy.start()
    for t in range(frames):
        for copy in stores(t):
            copy.wait()


def on_device(sizes, latent, gain_first, bias_first, kernel_first, gain_second, bias_second, kernel_second, conv_bias):
    n_tm, n_row, n_col = sizes
    frames, rows, cols, channels = latent.shape
    plane = n_row * n_col
    per_span = float(frames * rows * n_row * cols * n_col * (channels // GROUPS))
    tile = (frames + 2, rows + 2, cols, channels)
    tall = -(-(rows + 2) // 8) * 8
    cells = (2, frames + 2, tall, channels)
    send = (2, frames, tall, channels)
    taps = (27, channels, channels)
    anywhere = pl.BlockSpec(memory_space=pltpu.HBM)
    inside = pl.BlockSpec(memory_space=pltpu.VMEM)
    kept = [
        pltpu.VMEM(tile, BF16),
        pltpu.VMEM(tile, BF16),
        pltpu.VMEM(cells, BF16),
        pltpu.VMEM(taps, BF16),
        pltpu.VMEM((8, channels), F32),
    ]
    held = pl.pallas_call(
        functools.partial(first_kernel, sizes, per_span),
        out_shape=kept,
        in_specs=[anywhere] * 7,
        out_specs=[inside] * 5,
        scratch_shapes=[
            pltpu.VMEM((3, *tile), BF16),
            pltpu.VMEM(taps, BF16),
            pltpu.VMEM(cells, BF16),
            pltpu.VMEM(send, BF16),
            pltpu.VMEM(send, BF16),
            pltpu.VMEM((2, tall, channels), F32),
            pltpu.VMEM((tall, channels), F32),
            pltpu.VMEM((4, 1, channels), F32),
            pltpu.VMEM((8, channels), F32),
            pltpu.VMEM((2, 1, 128), F32),
            pltpu.VMEM((2, plane - 1, 1, 128), F32),
            pltpu.VMEM((2, 1, 128), F32),
            pltpu.VMEM((2, n_tm - 1, 1, 128), F32),
            pltpu.SemaphoreType.DMA((7,)),
            pltpu.SemaphoreType.DMA((N_COPIES,)),
            pltpu.SemaphoreType.DMA((N_COPIES,)),
            pltpu.SemaphoreType.DMA((4,)),
            pltpu.SemaphoreType.DMA((4,)),
        ],
        compiler_params=pltpu.CompilerParams(
            collective_id=0, has_side_effects=True, vmem_limit_bytes=24 * 2**20
        ),
        name="first_conv",
    )(
        *(
            pltpu.with_memory_space_constraint(x, pltpu.HBM)
            for x in (
                latent,
                kernel_first.reshape(taps),
                kernel_second.reshape(taps),
                gain_first.reshape(1, channels),
                bias_first.reshape(1, channels),
                gain_second.reshape(1, channels),
                bias_second.reshape(1, channels),
            )
        )
    )
    out = pl.pallas_call(
        functools.partial(second_kernel, sizes),
        out_shape=jax.ShapeDtypeStruct((frames, rows, 2, 2 * cols, channels), BF16),
        in_specs=[inside] * 6,
        out_specs=anywhere,
        scratch_shapes=[
            pltpu.VMEM((3, *tile), BF16),
            pltpu.VMEM((2, tall, channels), F32),
            pltpu.VMEM((2, 2, 2 * rows * cols, 128), F32),
            pltpu.VMEM((frames, rows, 2 * cols, channels), BF16),
            pltpu.SemaphoreType.DMA((frames, 2)),
        ],
        compiler_params=pltpu.CompilerParams(vmem_limit_bytes=24 * 2**20),
        name="second_conv",
    )(*held, conv_bias.reshape(1, channels))
    return out.reshape(frames, 2 * rows, 2 * cols, channels)


def solution(mesh):
    sizes = (mesh.shape["tm"], mesh.shape["row"], mesh.shape["col"])
    return jax.shard_map(
        functools.partial(on_device, sizes),
        mesh=mesh,
        in_specs=(P("tm", "row", "col", None), P(), P(), P(), P(), P(), P(), P()),
        out_specs=P("tm", "row", "col", None),
        check_vma=False,
    )
```
